256 devices in a mesh: ctx: 128 (over y, x, z), head: 2 (over core).
Axes of the slice: x: 4, y: 4, z: 8, core: 2. Of those that a mesh axis runs over, the one named last changes fastest.
Arguments:
- queries: bfloat16 [16384, 64, 128], P('ctx', 'head'), may hold values from -90 to 90
- key_heads: bfloat16 [16384, 8, 128], P('ctx', 'head'), may hold values from -4 to 4
- value_head_rows: bfloat16 [16384, 8, 128], P('ctx', 'head'), may hold values from -6 to 6
- doc_lengths: int32 [64], replicated, may hold values from 1 to 512, 16384 in all
Outputs:
- attended: bfloat16 [16384, 64, 128], P(('ctx', 'head'))
The draws below stay inside these ranges and needn't reach their ends.
Inputs may be any that keep to these rules, and one draw needn't show every extreme that they name: `doc_lengths`: lengths of 64 documents in order, summing to 16384; the longest is exactly 512.
All inputs are finite; a program needn't handle non-finite values.
Results may differ from the reference program's by a relative error of at most 0.0055.
Values may be sent and summed in bfloat16 or wider, within the bound.
A program may use at most 128 MiB of HBM per device.

```python
import math
import jax
import jax.numpy as jnp
import numpy as np
from jax import lax

QUERY_HEADS = 64
KEY_VALUE_HEADS = 8
HEAD_WIDTH_SIZE = 128
BLOCK_TOKENS = 64
REACH_LOG = 3
SEQUENCE_TOKENS = 16384
LONGEST_DOCUMENT = 512
NDOC = 64
N_CTX = 128


def paired_draw(key):
    random_keys = jax.random.fold_in(key, 11)
    random_queries = jax.random.fold_in(key, 23)
    key_entries = jnp.clip(jax.random.normal(random_keys, (SEQUENCE_TOKENS, KEY_VALUE_HEADS, HEAD_WIDTH_SIZE), jnp.float32), -4.0, 4.0)
    query_entries = jnp.clip(jax.random.normal(random_queries, (SEQUENCE_TOKENS, QUERY_HEADS, HEAD_WIDTH_SIZE), jnp.float32), -4.0, 4.0)
    return (query_entries, key_entries)


def draw_queries(key, part):
    return paired_draw(key)[0].astype(jnp.bfloat16)


def draw_key_heads(key, part):
    return paired_draw(key)[1].astype(jnp.bfloat16)


def block_levels(own_key, extent, pieces, least, top_value):
    gain = 1.0
    for position, blocks in pieces:
        steps = jax.random.uniform(jax.random.fold_in(jax.random.fold_in(own_key, 6), position), (blocks,), jnp.float32, least / len(pieces), top_value / len(pieces))
        gain = gain * jnp.repeat(jnp.exp(steps), extent[position] // blocks).reshape((-1,) + (1,) * (len(extent) - 1 - position))
    return gain


def split_up(amount, total, reach, lean):
    portions = [(1 << 20) // math.isqrt(rank ** lean) + 1 for rank in range(2, amount + 1)]
    spare, holding = total - reach - (amount - 1), [1] * (amount - 1)
    while spare > 0:
        free = [i for i in range(amount - 1) if holding[i] < reach]
        pool, left = sum([portions[i] for i in free]), spare
        for i in free:
            extra = min(reach - holding[i], max(1, left * portions[i] // pool), spare)
            holding[i] = holding[i] + extra
            spare = spare - extra
    return np.array([reach] + holding)


def uneven(rng, number_of, total, most, skew):
    if number_of == 2:
        one = jax.random.randint(rng, (), max(1, total - most), min(most, total - 1) + 1)
        return jnp.stack([one, total - one])
    lengths = jnp.asarray(split_up(number_of, total, most, skew), jnp.int32)
    pairs = (number_of - 1) // 2
    source_of, receiver = lengths[1:1 + 2 * pairs:2], lengths[2:2 + 2 * pairs:2]
    margin = jnp.minimum(source_of - 1, most - receiver)
    passed = jax.random.randint(jax.random.fold_in(rng, 1), (pairs,), 0, 1 << 20) % (margin + 1)
    lengths = lengths.at[1:1 + 2 * pairs:2].set(source_of - passed).at[2:2 + 2 * pairs:2].set(receiver + passed)
    return lengths[jax.random.permutation(jax.random.fold_in(rng, 2), number_of)]


def normal_values(rng, extent, spread, most, shards=(), held_as=jnp.bfloat16):
    entries = jax.random.normal(rng, extent, jnp.float32) * spread
    if len(shards) > 0:
        entries = block_levels(rng, extent, shards, -0.22, 0.18) * entries
    return jnp.clip(entries, min=-most, max=most).astype(held_as)


def setup_inputs(seed: int = 0) -> dict:
    splits = jax.random.split(jax.random.key(seed), 5)
    return {
        "queries": draw_queries(jax.random.fold_in(splits[4], 71), 0),
        "key_heads": draw_key_heads(jax.random.fold_in(splits[4], 71), 0),
        "value_head_rows": normal_values(splits[2], (SEQUENCE_TOKENS, KEY_VALUE_HEADS, HEAD_WIDTH_SIZE), 1.0, 6.0, ((0, 128), (1, 2))),
        "doc_lengths": uneven(splits[3], NDOC, SEQUENCE_TOKENS, LONGEST_DOCUMENT, 2).astype(jnp.int32),
    }


MASKED_SCORE = -1.0e30


def natural_rows():
    places = jnp.arange(SEQUENCE_TOKENS, dtype=jnp.int32)
    stretch_idx = places // BLOCK_TOKENS
    in_stretch = places % BLOCK_TOKENS
    lower = stretch_idx < N_CTX
    device = jnp.where(lower, stretch_idx, 2 * N_CTX - 1 - stretch_idx)
    offset = jnp.where(lower, in_stretch, BLOCK_TOKENS + in_stretch)
    return (device * (2 * BLOCK_TOKENS) + offset).astype(jnp.int32)


def reference(queries, key_heads, value_head_rows, doc_lengths):
    row_ids = natural_rows()
    query_order = queries[row_ids]
    key_folded_rows = key_heads[row_ids]
    value_folded_rows = value_head_rows[row_ids]
    places = jnp.arange(SEQUENCE_TOKENS, dtype=jnp.int32)
    doc_ends = jnp.cumsum(doc_lengths).astype(jnp.int32)
    doc_starts = (doc_ends - doc_lengths).astype(jnp.int32)
    doc_order = jnp.sum((places[:, None] >= doc_ends[None, :]).astype(jnp.int32), axis=1).astype(jnp.int32)
    total_tiles = 2 ** REACH_LOG + 1
    visible_span = total_tiles * BLOCK_TOKENS
    query_group = QUERY_HEADS // KEY_VALUE_HEADS
    score_scale = 1.0 / (HEAD_WIDTH_SIZE ** 0.5)
    padded_keys = jnp.concatenate([jnp.zeros((LONGEST_DOCUMENT, KEY_VALUE_HEADS, HEAD_WIDTH_SIZE), key_folded_rows.dtype), key_folded_rows], axis=0)
    padded_values = jnp.concatenate([jnp.zeros((LONGEST_DOCUMENT, KEY_VALUE_HEADS, HEAD_WIDTH_SIZE), value_folded_rows.dtype), value_folded_rows], axis=0)
    doc_padded = jnp.concatenate([jnp.full((LONGEST_DOCUMENT,), -1, jnp.int32), doc_order], axis=0)

    def one_block(index):
        begin = (index * BLOCK_TOKENS).astype(jnp.int32)
        query_block = lax.dynamic_slice_in_dim(query_order, begin, BLOCK_TOKENS, 0).astype(jnp.float32)
        query_block = query_block.reshape(BLOCK_TOKENS, KEY_VALUE_HEADS, query_group, HEAD_WIDTH_SIZE)
        q_doc = lax.dynamic_slice_in_dim(doc_order, begin, BLOCK_TOKENS, 0)
        q_place = begin + jnp.arange(BLOCK_TOKENS, dtype=jnp.int32)
        first_start = jnp.sum(jnp.where(jnp.arange(NDOC, dtype=jnp.int32) == q_doc[0], doc_starts, 0)).astype(jnp.int32)
        leading_tile = ((first_start - begin + LONGEST_DOCUMENT) // BLOCK_TOKENS).astype(jnp.int32)

        def score_tile(tile, holding_array):
            start = (begin + tile * BLOCK_TOKENS).astype(jnp.int32)
            k_tile = lax.dynamic_slice_in_dim(padded_keys, start, BLOCK_TOKENS, 0).astype(jnp.float32)
            key_doc = lax.dynamic_slice_in_dim(doc_padded, start, BLOCK_TOKENS, 0)
            key_place = start - LONGEST_DOCUMENT + jnp.arange(BLOCK_TOKENS, dtype=jnp.int32)
            allowed = (q_doc[:, None] == key_doc[None, :]) & (key_place[None, :] <= q_place[:, None])
            scores = jnp.einsum("qkgd,tkd->kgqt", query_block, k_tile) * score_scale
            scores = jnp.where(allowed, scores, MASKED_SCORE)
            return lax.dynamic_update_slice_in_dim(holding_array, scores, (tile * BLOCK_TOKENS).astype(jnp.int32), 3)

        holding_array = jnp.full((KEY_VALUE_HEADS, query_group, BLOCK_TOKENS, visible_span), MASKED_SCORE, jnp.float32)
        holding_array = lax.fori_loop(leading_tile, total_tiles, score_tile, holding_array)
        live = holding_array > 0.5 * MASKED_SCORE
        largest = jnp.max(holding_array, axis=-1, keepdims=True)
        weights = jnp.where(live, jnp.exp(holding_array - largest), 0.0)
        totals = jnp.sum(weights, axis=-1)
        rounded = lax.optimization_barrier(weights.astype(jnp.bfloat16)).astype(jnp.float32)

        def combine_tile(tile, total):
            start = (begin + tile * BLOCK_TOKENS).astype(jnp.int32)
            v_tile = lax.dynamic_slice_in_dim(padded_values, start, BLOCK_TOKENS, 0).astype(jnp.float32)
            w_tile = lax.dynamic_slice_in_dim(rounded, (tile * BLOCK_TOKENS).astype(jnp.int32), BLOCK_TOKENS, 3)
            return total + jnp.einsum("kgqt,tkd->kgqd", w_tile, v_tile)

        combined_output = lax.fori_loop(leading_tile, total_tiles, combine_tile, jnp.zeros((KEY_VALUE_HEADS, query_group, BLOCK_TOKENS, HEAD_WIDTH_SIZE), jnp.float32))
        result = combined_output / totals[..., None]
        result = jnp.transpose(result, (2, 0, 1, 3)).reshape(BLOCK_TOKENS, QUERY_HEADS, HEAD_WIDTH_SIZE)
        return result.astype(jnp.bfloat16)

    blocks = lax.map(one_block, jnp.arange(SEQUENCE_TOKENS // BLOCK_TOKENS, dtype=jnp.int32))
    natural = blocks.reshape(SEQUENCE_TOKENS, QUERY_HEADS, HEAD_WIDTH_SIZE)
    return jnp.zeros((SEQUENCE_TOKENS, QUERY_HEADS, HEAD_WIDTH_SIZE), jnp.bfloat16).at[row_ids].set(natural)
```

```python
import functools
import math

import jax
import jax.numpy as jnp
from jax import lax
from jax.experimental import pallas as pl
from jax.experimental.pallas import tpu as pltpu
from jax.sharding import PartitionSpec as P

REACH = 8
MASKED = -1e30
MESH = pl.DeviceIdType.MESH


def kernel(
    ctx_count,
    q_hbm,
    k_hbm,
    v_hbm,
    len_hbm,
    o_hbm,
    q_scr,
    kv,
    kv_out,
    raw,
    wide,
    bias,
    acc,
    total,
    largest,
    o_scr,
    lens,
    raw_sem,
    len_sem,
    q_sem,
    q_send_sem,
    o_sem,
    recv_sem,
    send_sem,
    pair_sem,
):
    kv_heads = k_hbm.shape[1]
    group = q_hbm.shape[1] // kv_heads
    rows = k_hbm.shape[0] // 2
    width = k_hbm.shape[2]
    docs = len_hbm.shape[0]
    nodes = 2 * ctx_count
    scale = math.log2(math.e) / math.sqrt(width)

    chip = lax.axis_index("ctx")
    core = lax.axis_index("head")
    other = 1 - core
    node = jnp.where(core == 0, chip, nodes - 1 - chip)

    def device(n):
        n = lax.rem(n + nodes, nodes)
        return (jnp.where(n < ctx_count, n, nodes - 1 - n), jnp.where(n < ctx_count, 0, 1))

    pair = (chip, other)
    above, below = device(node + 1), device(node - 1)
    far, far_back = device(node + REACH), device(node - REACH)

    local = []
    for part, half in enumerate((core, other)):
        for which, source in enumerate((k_hbm, v_hbm)):
            copy = pltpu.make_async_copy(
                source.at[pl.ds(pl.multiple_of(half * rows, rows), rows)],
                raw.at[part, which],
                raw_sem.at[part, which],
            )
            copy.start()
            local.append(copy)
    len_copy = pltpu.make_async_copy(len_hbm, lens, len_sem)
    len_copy.start()
    q_local, q_remote = [], []
    for k in range(kv_heads):
        copy = pltpu.make_async_copy(
            q_hbm.at[pl.ds(pl.multiple_of(core * rows, rows), rows), pl.ds(k * group, group)],
            q_scr.at[core * kv_heads + k],
            q_sem.at[core, k],
        )
        copy.start()
        q_local.append(copy)
        q_remote.append(
            pltpu.make_async_remote_copy(
                src_ref=q_hbm.at[
                    pl.ds(pl.multiple_of(other * rows, rows), rows), pl.ds(k * group, group)
                ],
                dst_ref=q_scr.at[core * kv_heads + k],
                send_sem=q_send_sem.at[k],
                recv_sem=q_sem.at[core, k],
                device_id=pair,
                device_id_type=MESH,
            )
        )

    barrier = pltpu.get_barrier_semaphore()
    for target in (pair, above, below, far_back):
        pl.semaphore_signal(barrier, inc=1, device_id=target, device_id_type=MESH)

    for part in (1, 0):
        for which in range(2):
            local[2 * part + which].wait()
            wide[...] = raw[part, which].astype(jnp.float32)
            for k in range(kv_heads):
                piece = wide.reshape(rows * kv_heads, width)[
                    pl.ds(k, rows, stride=kv_heads), :
                ].astype(jnp.bfloat16)
                if part == 0:
                    kv[0, core, k, which] = piece
                else:
                    kv_out[k, which] = piece

    pl.semaphore_wait(barrier, 4)

    def to_pair():
        return pltpu.make_async_remote_copy(
            src_ref=kv_out,
            dst_ref=kv.at[0, core],
            send_sem=pair_sem,
            recv_sem=recv_sem.at[0, core],
            device_id=pair,
            device_id_type=MESH,
        )

    def send(slot, into, half, target):
        return pltpu.make_async_remote_copy(
            src_ref=kv.at[slot, half],
            dst_ref=kv.at[into, half],
            send_sem=send_sem.at[into, half],
            recv_sem=recv_sem.at[into, half],
            device_id=target,
            device_id_type=MESH,
        )

    def incoming(slot, half):
        return send(slot, slot, half, above)

    to_pair().start()
    send(0, 1, core, above).start()
    send(0, REACH, core, far).start()
    for copy in q_remote:
        copy.start()

    len_copy.wait()
    lane = lax.broadcasted_iota(jnp.int32, (8, 128), 1)

    def add_doc(j, ends):
        return ends + jnp.where(lane >= j, lens[j], 0)

    ends = lax.fori_loop(0, docs, add_doc, jnp.zeros((8, 128), jnp.int32))
    ends = jnp.where(lane < docs, ends, 0)
    ends = jnp.concatenate([ends] * rows, axis=0)
    row = lax.broadcasted_iota(jnp.int32, (rows * group, 128), 0) // group
    column = lax.broadcasted_iota(jnp.int32, (rows * group, 128), 1)
    place = node * rows + row
    begin = jnp.max(jnp.where(ends <= place, ends, 0), axis=1, keepdims=True)

    send_second = [send(0, 1, other, above), send(0, REACH, other, far)]
    incoming(0, other).wait_recv()
    for copy in send_second:
        copy.start()

    for step in range(REACH // 2 + 1):
        near, away = (0, 0) if step == 0 else (step, REACH + 1 - step)
        back = jnp.where(column < rows, near, away)
        seen = (node - back) * rows + column % rows
        allowed = (seen >= begin) & (seen <= place)
        if step == 0:
            allowed = allowed & (column < rows)
        bias[step] = jnp.where(allowed, 0.0, MASKED)

    def attend(step, half):
        slots = (0,) if step == 0 else (step, REACH + 1 - step)
        last = step == REACH // 2
        lanes = rows * len(slots)

        def one_head(k, carry):
            head = half * kv_heads + k
            queries = q_scr.reshape(2 * kv_heads, rows * group, width)[head]
            keys = jnp.concatenate([kv[s, half, k, 0] for s in slots], axis=0)
            values = jnp.concatenate([kv[s, half, k, 1] for s in slots], axis=0)
            scores = lax.dot_general(
                queries, keys, (((1,), (1,)), ((), ())), preferred_element_type=jnp.float32
            )
            scores = scores * scale + bias[step, :, :lanes]
            highest = jnp.max(scores, axis=1, keepdims=True)
            if step == 0:
                updated = jnp.broadcast_to(highest, (rows * group, width))
                weights = jnp.exp2(scores - updated[:, :lanes])
                sums = jnp.broadcast_to(
                    jnp.sum(weights, axis=1, keepdims=True), (rows * group, width)
                ) * (1.0 / width)
            else:
                earlier = largest[head]
                updated = jnp.maximum(earlier, highest)
                shrink = jnp.exp2(earlier - updated)
                weights = jnp.exp2(scores - updated)
                sums = total[head] * shrink + weights
            out = jnp.dot(
                weights.astype(jnp.bfloat16), values, preferred_element_type=jnp.float32
            )
            if step > 0:
                out = acc[head] * shrink + out
            if last:
                result = out * (1.0 / jnp.sum(sums, axis=1, keepdims=True))
                o_scr.reshape(2 * kv_heads, rows * group, width)[head] = result.astype(
                    jnp.bfloat16
                )
                write(head).start()
            else:
                acc[head] = out
                total[head] = sums
                largest[head] = updated
            return carry

        lax.fori_loop(0, kv_heads, one_head, 0)

    def write(head):
        return pltpu.make_async_copy(
            o_scr.at[head],
            o_hbm.at[:, pl.ds(pl.multiple_of(head * group, group), group)],
            o_sem.at[head],
        )

    def wait_queries(half, copies):
        for copy in copies:
            copy.wait() if half is core else copy.wait_recv()

    def forward(step, half):
        incoming(step, half).wait_recv()
        if step < REACH // 2:
            send(step, step + 1, half, above).start()
        incoming(REACH + 1 - step, half).wait_recv()
        if step < REACH // 2:
            send(REACH + 1 - step, REACH - step, half, below).start()

    q_arriving = [
        pltpu.make_async_remote_copy(
            src_ref=q_scr.at[other * kv_heads + k],
            dst_ref=q_scr.at[other * kv_heads + k],
            send_sem=q_send_sem.at[k],
            recv_sem=q_sem.at[other, k],
            device_id=pair,
            device_id_type=MESH,
        )
        for k in range(kv_heads)
    ]
    wait_queries(core, q_local)
    attend(0, core)
    forward(1, core)
    wait_queries(other, q_arriving)
    attend(0, other)
    forward(1, other)
    for step in range(1, REACH // 2 + 1):
        attend(step, core)
        if step < REACH // 2:
            forward(step + 1, core)
        attend(step, other)
        if step < REACH // 2:
            forward(step + 1, other)

    to_pair().wait_send()
    for copy in q_remote:
        copy.wait_send()
    for into in range(1, REACH + 1):
        for half in range(2):
            send(0, into, half, above).wait_send()
    for head in range(2 * kv_heads):
        write(head).wait()


def shards(queries, key_heads, value_head_rows, doc_lengths):
    kv_heads = key_heads.shape[1]
    rows = key_heads.shape[0] // 2
    width = key_heads.shape[2]
    group = queries.shape[1] // kv_heads
    heads = 2 * kv_heads
    half_steps = REACH // 2 + 1
    any_space = pl.BlockSpec(memory_space=pl.ANY)
    state = pltpu.VMEM((heads, rows * group, width), jnp.float32)
    return pl.pallas_call(
        functools.partial(kernel, lax.axis_size("ctx")),
        name="relay_attention",
        out_shape=jax.ShapeDtypeStruct((rows, heads * group, width), jnp.bfloat16),
        in_specs=[any_space] * 4,
        out_specs=any_space,
        scratch_shapes=[
            pltpu.VMEM((heads, rows, group, width), jnp.bfloat16),
            pltpu.VMEM((REACH + 1, 2, kv_heads, 2, rows, width), jnp.bfloat16),
            pltpu.VMEM((kv_heads, 2, rows, width), jnp.bfloat16),
            pltpu.VMEM((2, 2, rows, kv_heads, width), jnp.bfloat16),
            pltpu.VMEM((rows, kv_heads, width), jnp.float32),
            pltpu.VMEM((half_steps, rows * group, 128), jnp.float32),
            state,
            state,
            state,
            pltpu.VMEM((heads, rows, group, width), jnp.bfloat16),
            pltpu.SMEM(doc_lengths.shape, jnp.int32),
            pltpu.SemaphoreType.DMA((2, 2)),
            pltpu.SemaphoreType.DMA,
            pltpu.SemaphoreType.DMA((2, kv_heads)),
            pltpu.SemaphoreType.DMA((kv_heads,)),
            pltpu.SemaphoreType.DMA((heads,)),
            pltpu.SemaphoreType.DMA((REACH + 1, 2)),
            pltpu.SemaphoreType.DMA((REACH + 1, 2)),
            pltpu.SemaphoreType.DMA,
        ],
        compiler_params=pltpu.CompilerParams(
            collective_id=0, has_side_effects=True, vmem_limit_bytes=40 << 20
        ),
    )(queries, key_heads, value_head_rows, doc_lengths)


def solution(mesh):
    in_specs = (P("ctx", "head", None), P("ctx", "head", None), P("ctx", "head", None), P())
    out_specs = P(("ctx", "head"), None, None)
    return jax.shard_map(shards, mesh=mesh, in_specs=in_specs, out_specs=out_specs, check_vma=False)
```

```python
import functools
import math

import jax
import jax.numpy as jnp
from jax import lax
from jax.experimental import pallas as pl
from jax.experimental.pallas import tpu as pltpu
from jax.sharding import PartitionSpec as P

REACH = 8
MASKED = -1e30
PIECES = 4
MESH = pl.DeviceIdType.MESH

USUAL = (1, 8, 2, 7, 3, 6, 4, 5)
AT_FOLD = (
    USUAL,
    (3, 1, 2, 4, 5, 6, 8, 7),
    (5, 1, 4, 6, 2, 3, 7, 8),
    (7, 1, 6, 8, 2, 5, 3, 4),
    USUAL,
    (1, 2, 3, 5, 6, 8, 4, 7),
    (1, 2, 6, 7, 3, 5, 8, 4),
    USUAL,
)


def kernel(
    ctx_count,
    q_hbm,
    k_hbm,
    v_hbm,
    len_hbm,
    o_hbm,
    q_scr,
    q_turned,
    kv,
    kv_out,
    raw,
    wide,
    bias,
    acc,
    total,
    largest,
    o_scr,
    lens,
    raw_sem,
    len_sem,
    q_sem,
    q_send_sem,
    o_sem,
    recv_sem,
    send_sem,
    pass_sem,
    pair_sem,
):
    kv_heads = k_hbm.shape[1]
    heads = 2 * kv_heads
    group = q_hbm.shape[1] // kv_heads
    rows = k_hbm.shape[0] // 2
    width = k_hbm.shape[2]
    docs = len_hbm.shape[0]
    tall = rows * group
    nodes = 2 * ctx_count
    own_pieces = PIECES // 2
    piece_heads = heads // PIECES
    depth = REACH // 2
    scale = math.log2(math.e) / math.sqrt(width)

    chip = lax.axis_index("ctx")
    core = lax.axis_index("head")
    other = 1 - core
    node = chip + core * (nodes - 1 - 2 * chip)
    ring, spot = lax.div(node, REACH), lax.rem(node, REACH)
    rings = ctx_count // REACH
    along = lax.rem(ring, rings)
    folds = lax.div(along + 1, rings)
    folded = 1 - lax.div(along + rings - 1, rings)

    def device(n):
        leg = lax.div(n, ctx_count)
        return (n + leg * (nodes - 1 - 2 * n), leg)

    pair = (chip, other)
    above = device(ring * REACH + lax.rem(spot + 1, REACH))
    below = device(ring * REACH + lax.rem(spot + REACH - 1, REACH))
    opposite = nodes - 1 - node
    after = device(folds * opposite + (1 - folds) * lax.rem(node + REACH, nodes))
    before = device(folded * opposite + (1 - folded) * lax.rem(node + nodes - REACH, nodes))
    spot_after = spot + folds * (REACH - 1 - 2 * spot)

    def equal(a, b):
        return 1 - lax.div((a - b) * (a - b) + 63, 64)

    order = []
    for i in range(REACH):
        change = sum(
            equal(spot, place) * (AT_FOLD[place][i] - USUAL[i])
            for place in range(REACH)
            if AT_FOLD[place][i] != USUAL[i]
        )
        order.append(USUAL[i] + folded * change)

    local = []
    for part, half in enumerate((core, other)):
        for which, source in enumerate((k_hbm, v_hbm)):
            copy = pltpu.make_async_copy(
                source.at[pl.ds(pl.multiple_of(half * rows, rows), rows)],
                raw.at[part, which],
                raw_sem.at[part, which],
            )
            copy.start()
            local.append(copy)
    len_copy = pltpu.make_async_copy(len_hbm, lens, len_sem)
    len_copy.start()
    q_local, q_remote = [], []
    for k in range(kv_heads):
        copy = pltpu.make_async_copy(
            q_hbm.at[pl.ds(pl.multiple_of(core * rows, rows), rows), pl.ds(k * group, group)],
            q_scr.at[core * kv_heads + k],
            q_sem.at[core, k],
        )
        copy.start()
        q_local.append(copy)
        q_remote.append(
            pltpu.make_async_remote_copy(
                src_ref=q_hbm.at[
                    pl.ds(pl.multiple_of(other * rows, rows), rows), pl.ds(k * group, group)
                ],
                dst_ref=q_scr.at[core * kv_heads + k],
                send_sem=q_send_sem.at[k],
                recv_sem=q_sem.at[core, k],
                device_id=pair,
                device_id_type=MESH,
            )
        )

    barrier = pltpu.get_barrier_semaphore()
    for target in (pair, above, below, before):
        pl.semaphore_signal(barrier, inc=1, device_id=target, device_id_type=MESH)

    for part in (1, 0):
        for which in range(2):
            local[2 * part + which].wait()
            wide[...] = raw[part, which].astype(jnp.float32)
            for k in range(kv_heads):
                block = wide.reshape(rows * kv_heads, width)[
                    pl.ds(k, rows, stride=kv_heads), :
                ].astype(jnp.bfloat16)
                piece, head = k // piece_heads, k % piece_heads
                if part == 0:
                    kv[0, core * own_pieces + piece, head, which] = block
                else:
                    kv_out[piece, head, which] = block

    pl.semaphore_wait(barrier, 4)

    def to_pair(i):
        return pltpu.make_async_remote_copy(
            src_ref=kv_out.at[i],
            dst_ref=kv.at[0, core * own_pieces + i],
            send_sem=pair_sem.at[i],
            recv_sem=recv_sem.at[0, core * own_pieces + i],
            device_id=pair,
            device_id_type=MESH,
        )

    def send(slot, into, piece, target):
        return pltpu.make_async_remote_copy(
            src_ref=kv.at[slot, piece],
            dst_ref=kv.at[into, piece],
            send_sem=send_sem.at[into, piece],
            recv_sem=recv_sem.at[into, piece],
            device_id=target,
            device_id_type=MESH,
        )

    def incoming(slot, piece):
        return pltpu.make_async_remote_copy(
            src_ref=kv.at[slot, piece],
            dst_ref=kv.at[slot, piece],
            send_sem=pair_sem.at[0],
            recv_sem=recv_sem.at[slot, piece],
            device_id=above,
            device_id_type=MESH,
        )

    def pass_on(slot, piece):
        source = lax.rem(spot - slot + REACH, REACH)
        lacking = lax.div(source - spot_after + REACH, REACH)
        into = 2 * REACH - 1 - lacking * (source - spot_after)
        copy = pltpu.make_async_remote_copy(
            src_ref=kv.at[slot, piece],
            dst_ref=kv.at[into, piece],
            send_sem=pass_sem.at[slot, piece],
            recv_sem=recv_sem.at[into, piece],
            device_id=after,
            device_id_type=MESH,
        )
        return lacking == 1, copy

    def start_pass(slot, piece):
        lacking, copy = pass_on(slot, piece)
        pl.when(lacking)(copy.start)

    def first_sends(piece):
        send(0, 1, piece, above).start()
        send(0, REACH - 1, piece, below).start()
        start_pass(0, piece)

    def piece_at(i):
        half = lax.rem(core + lax.div(i, own_pieces), 2)
        return half * own_pieces + lax.rem(i, own_pieces)

    for i in range(own_pieces):
        to_pair(i).start()
    for i in range(own_pieces):
        first_sends(core * own_pieces + i)
    for copy in q_remote:
        copy.start()
    for i in range(own_pieces):
        incoming(0, other * own_pieces + i).wait_recv()
        first_sends(other * own_pieces + i)

    len_copy.wait()
    place = node * rows + lax.broadcasted_iota(jnp.int32, (8, tall), 1) // group

    def add_doc(j, carry):
        end, begin = carry
        end = end + lens[j]
        return end, jnp.where(place >= end, end, begin)

    _, begin = lax.fori_loop(0, docs, add_doc, (jnp.int32(0), jnp.zeros((8, tall), jnp.int32)))

    backs = [(0, 0)] + [(order[2 * i], order[2 * i + 1]) for i in range(depth)]
    key_row = lax.broadcasted_iota(jnp.int32, (8, tall), 0)
    for step, both in enumerate(backs):
        for part in range(1 if step == 0 else 2):
            base = (node - both[part]) * rows

            def fill(i, carry, step=step, part=part, base=base):
                seen = base + i * 8 + key_row
                allowed = (seen >= begin) & (seen <= place)
                at = pl.multiple_of(part * rows + i * 8, 8)
                bias[step, pl.ds(at, 8), :] = jnp.where(allowed, 0.0, MASKED)
                return carry

            lax.fori_loop(0, rows // 8, fill, 0)

    def slot_of(back):
        return back + (REACH - 1) * lax.div(back - spot + REACH - 1, REACH)

    def write(head):
        return pltpu.make_async_copy(
            o_scr.at[head],
            o_hbm.at[:, pl.ds(pl.multiple_of(head * group, group), group)],
            o_sem.at[head],
        )

    def attend(step, piece, backs, last):
        first = not backs
        for back in backs:
            pl.when(back > spot)(incoming(REACH - 1 + back, piece).wait_recv)
        slots = [slot_of(back) for back in backs] or [0]
        depth_keys = rows * len(slots)
        for i in range(piece_heads):
            head = piece * piece_heads + i
            keys = jnp.concatenate([kv[s, piece, i, 0] for s in slots], axis=0)
            values = jnp.concatenate([kv[s, piece, i, 1] for s in slots], axis=0)
            scores = jnp.dot(keys, q_turned[head], preferred_element_type=jnp.float32)
            scores = scores * scale + bias[step, :depth_keys]
            updated = jnp.max(scores, axis=0, keepdims=True)
            if not first:
                earlier = largest[head]
                updated = jnp.maximum(earlier, updated)
                shrink = jnp.exp2(earlier - updated)
            weights = jnp.exp2(scores - updated)
            sums = jnp.sum(weights, axis=0, keepdims=True)
            out = lax.dot_general(
                values,
                weights.astype(jnp.bfloat16),
                (((0,), (0,)), ((), ())),
                preferred_element_type=jnp.float32,
            )
            if not first:
                sums = total[head] * shrink + sums
                out = acc[head] * shrink + out
            if last:
                result = (out * (1.0 / sums)).T.astype(jnp.bfloat16)
                o_scr.reshape(heads, tall, width)[head] = result
                write(head).start()
            else:
                acc[head] = out
                total[head] = sums
                largest[head] = updated

    def forward(step, piece):
        incoming(step, piece).wait_recv()
        pl.when(step < depth)(lambda: send(step, step + 1, piece, above).start())
        start_pass(step, piece)

        @pl.when(step < depth)
        def _():
            incoming(REACH - step, piece).wait_recv()
            pl.when(step < depth - 1)(
                lambda: send(REACH - step, REACH - step - 1, piece, below).start()
            )
            start_pass(REACH - step, piece)

    def turn(head):
        q_turned[head] = q_scr.reshape(heads, tall, width)[head].T

    for k in range(kv_heads):
        q_local[k].wait()
    for k in range(kv_heads):
        pltpu.make_async_remote_copy(
            src_ref=q_scr.at[other * kv_heads + k],
            dst_ref=q_scr.at[other * kv_heads + k],
            send_sem=q_send_sem.at[k],
            recv_sem=q_sem.at[other, k],
            device_id=pair,
            device_id_type=MESH,
        ).wait_recv()

    def begin_piece(i, carry):
        piece = piece_at(i)
        forward(1, piece)
        for k in range(piece_heads):
            turn(piece * piece_heads + k)
        attend(0, piece, (), False)
        return carry

    lax.fori_loop(0, PIECES, begin_piece, 0)

    def middle(i, carry):
        step, piece = lax.div(i, PIECES) + 1, piece_at(lax.rem(i, PIECES))
        forward(step + 1, piece)
        both = [
            sum(equal(step, at) * backs[at][part] for at in range(1, depth)) for part in range(2)
        ]
        attend(step, piece, both, False)
        return carry

    lax.fori_loop(0, (depth - 1) * PIECES, middle, 0)

    def finish_piece(i, carry):
        attend(depth, piece_at(i), backs[depth], True)
        return carry

    lax.fori_loop(0, PIECES, finish_piece, 0)

    for i in range(own_pieces):
        to_pair(i).wait_send()
    for copy in q_remote:
        copy.wait_send()
    for slot in range(REACH):
        for piece in range(PIECES):
            if slot > 0:
                send(0, slot, piece, above).wait_send()
            lacking, copy = pass_on(slot, piece)
            pl.when(lacking)(copy.wait_send)
    for head in range(heads):
        write(head).wait()


def shards(queries, key_heads, value_head_rows, doc_lengths):
    kv_heads = key_heads.shape[1]
    rows = key_heads.shape[0] // 2
    width = key_heads.shape[2]
    group = queries.shape[1] // kv_heads
    heads = 2 * kv_heads
    tall = rows * group
    piece = (heads // PIECES, 2, rows, width)
    steps = REACH // 2 + 1
    any_space = pl.BlockSpec(memory_space=pl.ANY)
    return pl.pallas_call(
        functools.partial(kernel, lax.axis_size("ctx")),
        name="relay_attention",
        out_shape=jax.ShapeDtypeStruct((rows, heads * group, width), jnp.bfloat16),
        in_specs=[any_space] * 4,
        out_specs=any_space,
        scratch_shapes=[
            pltpu.VMEM((heads, rows, group, width), jnp.bfloat16),
            pltpu.VMEM((heads, width, tall), jnp.bfloat16),
            pltpu.VMEM((2 * REACH, PIECES, *piece), jnp.bfloat16),
            pltpu.VMEM((PIECES // 2, *piece), jnp.bfloat16),
            pltpu.VMEM((2, 2, rows, kv_heads, width), jnp.bfloat16),
            pltpu.VMEM((rows, kv_heads, width), jnp.float32),
            pltpu.VMEM((steps, 2 * rows, tall), jnp.float32),
            pltpu.VMEM((heads, width, tall), jnp.float32),
            pltpu.VMEM((heads, 1, tall), jnp.float32),
            pltpu.VMEM((heads, 1, tall), jnp.float32),
            pltpu.VMEM((heads, rows, group, width), jnp.bfloat16),
            pltpu.SMEM(doc_lengths.shape, jnp.int32),
            pltpu.SemaphoreType.DMA((2, 2)),
            pltpu.SemaphoreType.DMA,
            pltpu.SemaphoreType.DMA((2, kv_heads)),
            pltpu.SemaphoreType.DMA((kv_heads,)),
            pltpu.SemaphoreType.DMA((heads,)),
            pltpu.SemaphoreType.DMA((2 * REACH, PIECES)),
            pltpu.SemaphoreType.DMA((REACH, PIECES)),
            pltpu.SemaphoreType.DMA((REACH, PIECES)),
            pltpu.SemaphoreType.DMA((PIECES // 2,)),
        ],
        compiler_params=pltpu.CompilerParams(
            collective_id=0, has_side_effects=True, vmem_limit_bytes=61 << 20
        ),
    )(queries, key_heads, value_head_rows, doc_lengths)


def solution(mesh):
    in_specs = (P("ctx", "head", None), P("ctx", "head", None), P("ctx", "head", None), P())
    out_specs = P(("ctx", "head"), None, None)
    return jax.shard_map(shards, mesh=mesh, in_specs=in_specs, out_specs=out_specs, check_vma=False)
```

```python
import functools
import math

import jax
import jax.numpy as jnp
from jax import lax
from jax.experimental import pallas as pl
from jax.experimental.pallas import tpu as pltpu
from jax.sharding import PartitionSpec as P

REACH = 8
MASKED = -1e30
PIECES = 4
MESH = pl.DeviceIdType.MESH

USUAL = (1, 8, 2, 7, 3, 6, 4, 5)
AT_FOLD = (
    USUAL,
    (3, 1, 2, 4, 5, 6, 8, 7),
    (5, 1, 4, 6, 2, 3, 7, 8),
    (7, 1, 6, 8, 2, 5, 3, 4),
    USUAL,
    (1, 2, 3, 5, 6, 8, 4, 7),
    (1, 2, 6, 7, 3, 5, 8, 4),
    USUAL,
)


def kernel(
    ctx_count,
    q_hbm,
    k_hbm,
    v_hbm,
    len_hbm,
    o_ref,
    q_scr,
    q_turned,
    kv,
    kv_out,
    raw,
    wide,
    bias,
    acc,
    total,
    largest,
    lens,
    raw_sem,
    len_sem,
    q_sem,
    q_send_sem,
    recv_sem,
    send_sem,
    pass_sem,
    pair_sem,
):
    kv_heads = k_hbm.shape[1]
    heads = 2 * kv_heads
    group = q_hbm.shape[1] // kv_heads
    rows = k_hbm.shape[0] // 2
    width = k_hbm.shape[2]
    docs = len_hbm.shape[0]
    tall = rows * group
    nodes = 2 * ctx_count
    own_pieces = PIECES // 2
    piece_heads = heads // PIECES
    depth = REACH // 2
    scale = math.log2(math.e) / math.sqrt(width)

    chip = lax.axis_index("ctx")
    core = lax.axis_index("head")
    other = 1 - core
    node = chip + core * (nodes - 1 - 2 * chip)
    ring, spot = lax.div(node, REACH), lax.rem(node, REACH)
    rings = ctx_count // REACH
    along = lax.rem(ring, rings)
    folds = lax.div(along + 1, rings)
    folded = 1 - lax.div(along + rings - 1, rings)

    def device(n):
        leg = lax.div(n, ctx_count)
        return (n + leg * (nodes - 1 - 2 * n), leg)

    pair = (chip, other)
    above = device(ring * REACH + lax.rem(spot + 1, REACH))
    below = device(ring * REACH + lax.rem(spot + REACH - 1, REACH))
    opposite = nodes - 1 - node
    after = device(folds * opposite + (1 - folds) * lax.rem(node + REACH, nodes))
    before = device(folded * opposite + (1 - folded) * lax.rem(node + nodes - REACH, nodes))
    spot_after = spot + folds * (REACH - 1 - 2 * spot)

    def equal(a, b):
        return 1 - lax.div((a - b) * (a - b) + 63, 64)

    order = []
    for i in range(REACH):
        change = sum(
            equal(spot, place) * (AT_FOLD[place][i] - USUAL[i])
            for place in range(REACH)
            if AT_FOLD[place][i] != USUAL[i]
        )
        order.append(USUAL[i] + folded * change)

    local = []
    for part, half in enumerate((core, other)):
        for which, source in enumerate((k_hbm, v_hbm)):
            copy = pltpu.make_async_copy(
                source.at[pl.ds(pl.multiple_of(half * rows, rows), rows)],
                raw.at[part, which],
                raw_sem.at[part, which],
            )
            copy.start()
            local.append(copy)
    len_copy = pltpu.make_async_copy(len_hbm, lens, len_sem)
    len_copy.start()
    q_local, q_remote = [], []
    for k in range(kv_heads):
        copy = pltpu.make_async_copy(
            q_hbm.at[pl.ds(pl.multiple_of(core * rows, rows), rows), pl.ds(k * group, group)],
            q_scr.at[core * kv_heads + k],
            q_sem.at[core, k],
        )
        copy.start()
        q_local.append(copy)
        q_remote.append(
            pltpu.make_async_remote_copy(
                src_ref=q_hbm.at[
                    pl.ds(pl.multiple_of(other * rows, rows), rows), pl.ds(k * group, group)
                ],
                dst_ref=q_scr.at[core * kv_heads + k],
                send_sem=q_send_sem.at[k],
                recv_sem=q_sem.at[core, k],
                device_id=pair,
                device_id_type=MESH,
            )
        )

    barrier = pltpu.get_barrier_semaphore()
    for target in (pair, above, below, before):
        pl.semaphore_signal(barrier, inc=1, device_id=target, device_id_type=MESH)

    for part in (1, 0):
        for which in range(2):
            local[2 * part + which].wait()
            wide[...] = raw[part, which].astype(jnp.float32)
            for k in range(kv_heads):
                block = wide.reshape(rows * kv_heads, width)[
                    pl.ds(k, rows, stride=kv_heads), :
                ].astype(jnp.bfloat16)
                piece, head = k // piece_heads, k % piece_heads
                if part == 0:
                    kv[0, core * own_pieces + piece, head, which] = block
                else:
                    kv_out[piece, head, which] = block

    pl.semaphore_wait(barrier, 4)

    def to_pair(i):
        return pltpu.make_async_remote_copy(
            src_ref=kv_out.at[i],
            dst_ref=kv.at[0, core * own_pieces + i],
            send_sem=pair_sem.at[i],
            recv_sem=recv_sem.at[0, core * own_pieces + i],
            device_id=pair,
            device_id_type=MESH,
        )

    def send(slot, into, piece, target):
        return pltpu.make_async_remote_copy(
            src_ref=kv.at[slot, piece],
            dst_ref=kv.at[into, piece],
            send_sem=send_sem.at[into, piece],
            recv_sem=recv_sem.at[into, piece],
            device_id=target,
            device_id_type=MESH,
        )

    def incoming(slot, piece):
        return pltpu.make_async_remote_copy(
            src_ref=kv.at[slot, piece],
            dst_ref=kv.at[slot, piece],
            send_sem=pair_sem.at[0],
            recv_sem=recv_sem.at[slot, piece],
            device_id=above,
            device_id_type=MESH,
        )

    def pass_on(slot, piece):
        source = lax.rem(spot - slot + REACH, REACH)
        lacking = lax.div(source - spot_after + REACH, REACH)
        into = 2 * REACH - 1 - lacking * (source - spot_after)
        copy = pltpu.make_async_remote_copy(
            src_ref=kv.at[slot, piece],
            dst_ref=kv.at[into, piece],
            send_sem=pass_sem.at[slot, piece],
            recv_sem=recv_sem.at[into, piece],
            device_id=after,
            device_id_type=MESH,
        )
        return lacking == 1, copy

    def start_pass(slot, piece):
        lacking, copy = pass_on(slot, piece)
        pl.when(lacking)(copy.start)

    def first_sends(piece):
        send(0, 1, piece, above).start()
        send(0, REACH - 1, piece, below).start()
        start_pass(0, piece)

    def piece_at(i):
        half = lax.rem(core + lax.div(i, own_pieces), 2)
        return half * own_pieces + lax.rem(i, own_pieces)

    for i in range(own_pieces):
        to_pair(i).start()
    for i in range(own_pieces):
        first_sends(core * own_pieces + i)
    for copy in q_remote:
        copy.start()
    for i in range(own_pieces):
        incoming(0, other * own_pieces + i).wait_recv()
        first_sends(other * own_pieces + i)

    len_copy.wait()
    place = node * rows + lax.broadcasted_iota(jnp.int32, (8, tall), 1) // group

    def add_doc(j, carry):
        end, begin = carry
        end = end + lens[j]
        return end, jnp.where(place >= end, end, begin)

    _, begin = lax.fori_loop(0, docs, add_doc, (jnp.int32(0), jnp.zeros((8, tall), jnp.int32)))

    backs = [(0, 0)] + [(order[2 * i], order[2 * i + 1]) for i in range(depth)]
    key_row = lax.broadcasted_iota(jnp.int32, (8, tall), 0)
    for step, both in enumerate(backs):
        for part in range(1 if step == 0 else 2):
            base = (node - both[part]) * rows

            def fill(i, carry, step=step, part=part, base=base):
                seen = base + i * 8 + key_row
                allowed = (seen >= begin) & (seen <= place)
                at = pl.multiple_of(part * rows + i * 8, 8)
                bias[step, pl.ds(at, 8), :] = jnp.where(allowed, 0.0, MASKED)
                return carry

            lax.fori_loop(0, rows // 8, fill, 0)

    def slot_of(back):
        return back + (REACH - 1) * lax.div(back - spot + REACH - 1, REACH)

    def attend(step, piece, backs, last):
        first = not backs
        for back in backs:
            pl.when(back > spot)(incoming(REACH - 1 + back, piece).wait_recv)
        slots = [slot_of(back) for back in backs] or [0]
        depth_keys = rows * len(slots)
        for i in range(piece_heads):
            head = piece * piece_heads + i
            keys = jnp.concatenate([kv[s, piece, i, 0] for s in slots], axis=0)
            values = jnp.concatenate([kv[s, piece, i, 1] for s in slots], axis=0)
            scores = jnp.dot(keys, q_turned[head], preferred_element_type=jnp.float32)
            scores = scores * scale + bias[step, :depth_keys]
            updated = jnp.max(scores, axis=0, keepdims=True)
            if not first:
                earlier = largest[head]
                updated = jnp.maximum(earlier, updated)
                shrink = jnp.exp2(earlier - updated)
            weights = jnp.exp2(scores - updated)
            sums = jnp.sum(weights, axis=0, keepdims=True)
            out = lax.dot_general(
                values,
                weights.astype(jnp.bfloat16),
                (((0,), (0,)), ((), ())),
                preferred_element_type=jnp.float32,
            )
            if not first:
                sums = total[head] * shrink + sums
                out = acc[head] * shrink + out
            if last:
                result = (out * (1.0 / sums)).T.reshape(rows, group, width).astype(jnp.bfloat16)
                o_ref[:, pl.ds(pl.multiple_of(head * group, group), group), :] = result
            else:
                acc[head] = out
                total[head] = sums
                largest[head] = updated

    def forward(step, piece):
        incoming(step, piece).wait_recv()
        pl.when(step < depth)(lambda: send(step, step + 1, piece, above).start())
        start_pass(step, piece)

        @pl.when(step < depth)
        def _():
            incoming(REACH - step, piece).wait_recv()
            pl.when(step < depth - 1)(
                lambda: send(REACH - step, REACH - step - 1, piece, below).start()
            )
            start_pass(REACH - step, piece)

    def turn(head):
        q_turned[head] = q_scr.reshape(heads, tall, width)[head].T

    for k in range(kv_heads):
        q_local[k].wait()
    for k in range(kv_heads):
        pltpu.make_async_remote_copy(
            src_ref=q_scr.at[other * kv_heads + k],
            dst_ref=q_scr.at[other * kv_heads + k],
            send_sem=q_send_sem.at[k],
            recv_sem=q_sem.at[other, k],
            device_id=pair,
            device_id_type=MESH,
        ).wait_recv()

    def begin_piece(i, carry):
        piece = piece_at(i)
        forward(1, piece)
        for k in range(piece_heads):
            turn(piece * piece_heads + k)
        attend(0, piece, (), False)
        return carry

    lax.fori_loop(0, PIECES, begin_piece, 0)

    def middle(i, carry):
        step, piece = lax.div(i, PIECES) + 1, piece_at(lax.rem(i, PIECES))
        forward(step + 1, piece)
        both = [
            sum(equal(step, at) * backs[at][part] for at in range(1, depth)) for part in range(2)
        ]
        attend(step, piece, both, False)
        return carry

    lax.fori_loop(0, (depth - 1) * PIECES, middle, 0)

    def finish_piece(i, carry):
        attend(depth, piece_at(i), backs[depth], True)
        return carry

    lax.fori_loop(0, PIECES, finish_piece, 0)

    for i in range(own_pieces):
        to_pair(i).wait_send()
    for copy in q_remote:
        copy.wait_send()
    for slot in range(REACH):
        for piece in range(PIECES):
            if slot > 0:
                send(0, slot, piece, above).wait_send()
            lacking, copy = pass_on(slot, piece)
            pl.when(lacking)(copy.wait_send)


def shards(queries, key_heads, value_head_rows, doc_lengths):
    queries, key_heads, value_head_rows, doc_lengths = (
        pltpu.with_memory_space_constraint(a, pltpu.HBM)
        for a in (queries, key_heads, value_head_rows, doc_lengths)
    )
    kv_heads = key_heads.shape[1]
    rows = key_heads.shape[0] // 2
    width = key_heads.shape[2]
    group = queries.shape[1] // kv_heads
    heads = 2 * kv_heads
    tall = rows * group
    piece = (heads // PIECES, 2, rows, width)
    steps = REACH // 2 + 1
    any_space = pl.BlockSpec(memory_space=pl.ANY)
    return pl.pallas_call(
        functools.partial(kernel, lax.axis_size("ctx")),
        name="relay_attention",
        out_shape=jax.ShapeDtypeStruct((rows, heads * group, width), jnp.bfloat16),
        in_specs=[any_space] * 4,
        out_specs=pl.BlockSpec(memory_space=pltpu.VMEM),
        scratch_shapes=[
            pltpu.VMEM((heads, rows, group, width), jnp.bfloat16),
            pltpu.VMEM((heads, width, tall), jnp.bfloat16),
            pltpu.VMEM((2 * REACH, PIECES, *piece), jnp.bfloat16),
            pltpu.VMEM((PIECES // 2, *piece), jnp.bfloat16),
            pltpu.VMEM((2, 2, rows, kv_heads, width), jnp.bfloat16),
            pltpu.VMEM((rows, kv_heads, width), jnp.float32),
            pltpu.VMEM((steps, 2 * rows, tall), jnp.float32),
            pltpu.VMEM((heads, width, tall), jnp.float32),
            pltpu.VMEM((heads, 1, tall), jnp.float32),
            pltpu.VMEM((heads, 1, tall), jnp.float32),
            pltpu.SMEM(doc_lengths.shape, jnp.int32),
            pltpu.SemaphoreType.DMA((2, 2)),
            pltpu.SemaphoreType.DMA,
            pltpu.SemaphoreType.DMA((2, kv_heads)),
            pltpu.SemaphoreType.DMA((kv_heads,)),
            pltpu.SemaphoreType.DMA((2 * REACH, PIECES)),
            pltpu.SemaphoreType.DMA((REACH, PIECES)),
            pltpu.SemaphoreType.DMA((REACH, PIECES)),
            pltpu.SemaphoreType.DMA((PIECES // 2,)),
        ],
        compiler_params=pltpu.CompilerParams(
            collective_id=0, has_side_effects=True, vmem_limit_bytes=32 << 20
        ),
    )(queries, key_heads, value_head_rows, doc_lengths)


def solution(mesh):
    in_specs = (P("ctx", "head", None), P("ctx", "head", None), P("ctx", "head", None), P())
    out_specs = P(("ctx", "head"), None, None)
    return jax.shard_map(shards, mesh=mesh, in_specs=in_specs, out_specs=out_specs, check_vma=False)
```

```python
import functools
import math

import jax
import jax.numpy as jnp
from jax import lax
from jax.experimental import pallas as pl
from jax.experimental.pallas import tpu as pltpu
from jax.sharding import PartitionSpec as P

REACH = 8
MASKED = -1e30
PIECES = 4
MESH = pl.DeviceIdType.MESH

USUAL = (1, 8, 2, 7, 3, 6, 4, 5)
AT_FOLD = (
    USUAL,
    (3, 1, 2, 4, 5, 6, 8, 7),
    (5, 1, 4, 6, 2, 3, 7, 8),
    (7, 1, 6, 8, 2, 5, 3, 4),
    USUAL,
    (1, 2, 3, 5, 6, 8, 4, 7),
    (1, 2, 6, 7, 3, 5, 8, 4),
    USUAL,
)


def kernel(
    ctx_count,
    q_hbm,
    k_hbm,
    v_hbm,
    len_hbm,
    o_ref,
    q_scr,
    q_turned,
    kv,
    kv_out,
    raw,
    wide,
    bias,
    acc,
    total,
    largest,
    lens,
    raw_sem,
    len_sem,
    q_sem,
    q_send_sem,
    recv_sem,
    send_sem,
    pass_sem,
    pair_sem,
):
    kv_heads = k_hbm.shape[1]
    heads = 2 * kv_heads
    group = q_hbm.shape[1] // kv_heads
    rows = k_hbm.shape[0] // 2
    width = k_hbm.shape[2]
    docs = len_hbm.shape[0]
    tall = rows * group
    nodes = 2 * ctx_count
    own_pieces = PIECES // 2
    piece_heads = heads // PIECES
    depth = REACH // 2
    scale = math.log2(math.e) / math.sqrt(width)

    chip = lax.axis_index("ctx")
    core = lax.axis_index("head")
    other = 1 - core
    node = chip + core * (nodes - 1 - 2 * chip)
    ring, spot = lax.div(node, REACH), lax.rem(node, REACH)
    rings = ctx_count // REACH
    along = lax.rem(ring, rings)
    folds = lax.div(along + 1, rings)
    folded = 1 - lax.div(along + rings - 1, rings)

    def device(n):
        leg = lax.div(n, ctx_count)
        return (n + leg * (nodes - 1 - 2 * n), leg)

    pair = (chip, other)
    above = device(ring * REACH + lax.rem(spot + 1, REACH))
    below = device(ring * REACH + lax.rem(spot + REACH - 1, REACH))
    opposite = nodes - 1 - node
    after = device(folds * opposite + (1 - folds) * lax.rem(node + REACH, nodes))
    before = device(folded * opposite + (1 - folded) * lax.rem(node + nodes - REACH, nodes))
    spot_after = spot + folds * (REACH - 1 - 2 * spot)

    def equal(a, b):
        return 1 - lax.div((a - b) * (a - b) + 63, 64)

    order = []
    for i in range(REACH):
        change = sum(
            equal(spot, place) * (AT_FOLD[place][i] - USUAL[i])
            for place in range(REACH)
            if AT_FOLD[place][i] != USUAL[i]
        )
        order.append(USUAL[i] + folded * change)

    local = []
    for part, half in enumerate((core, other)):
        for which, source in enumerate((k_hbm, v_hbm)):
            copy = pltpu.make_async_copy(
                source.at[pl.ds(pl.multiple_of(half * rows, rows), rows)],
                raw.at[part, which],
                raw_sem.at[part, which],
            )
            copy.start()
            local.append(copy)
    len_copy = pltpu.make_async_copy(len_hbm, lens, len_sem)
    len_copy.start()
    q_local, q_remote = [], []
    for k in range(kv_heads):
        copy = pltpu.make_async_copy(
            q_hbm.at[pl.ds(pl.multiple_of(core * rows, rows), rows), pl.ds(k * group, group)],
            q_scr.at[core * kv_heads + k],
            q_sem.at[core, k],
        )
        copy.start()
        q_local.append(copy)
        q_remote.append(
            pltpu.make_async_remote_copy(
                src_ref=q_hbm.at[
                    pl.ds(pl.multiple_of(other * rows, rows), rows), pl.ds(k * group, group)
                ],
                dst_ref=q_scr.at[core * kv_heads + k],
                send_sem=q_send_sem.at[k],
                recv_sem=q_sem.at[core, k],
                device_id=pair,
                device_id_type=MESH,
            )
        )

    barrier = pltpu.get_barrier_semaphore()
    for target in (pair, above, below, before):
        pl.semaphore_signal(barrier, inc=1, device_id=target, device_id_type=MESH)

    for part in (1, 0):
        for which in range(2):
            local[2 * part + which].wait()
            wide[...] = raw[part, which].astype(jnp.float32)
            for k in range(kv_heads):
                block = wide.reshape(rows * kv_heads, width)[
                    pl.ds(k, rows, stride=kv_heads), :
                ].astype(jnp.bfloat16)
                piece, head = k // piece_heads, k % piece_heads
                if part == 0:
                    kv[0, core * own_pieces + piece, head, which] = block
                else:
                    kv_out[piece, head, which] = block

    pl.semaphore_wait(barrier, 4)

    def to_pair(i):
        return pltpu.make_async_remote_copy(
            src_ref=kv_out.at[i],
            dst_ref=kv.at[0, core * own_pieces + i],
            send_sem=pair_sem,
            recv_sem=recv_sem.at[0, core * own_pieces + i],
            device_id=pair,
            device_id_type=MESH,
        )

    def send(slot, into, piece, target):
        return pltpu.make_async_remote_copy(
            src_ref=kv.at[slot, piece],
            dst_ref=kv.at[into, piece],
            send_sem=send_sem.at[into],
            recv_sem=recv_sem.at[into, piece],
            device_id=target,
            device_id_type=MESH,
        )

    def incoming(slot, piece):
        return pltpu.make_async_remote_copy(
            src_ref=kv.at[slot, piece],
            dst_ref=kv.at[slot, piece],
            send_sem=pair_sem,
            recv_sem=recv_sem.at[slot, piece],
            device_id=above,
            device_id_type=MESH,
        )

    def passing(slot):
        source = lax.rem(spot - slot + REACH, REACH)
        lacking = lax.div(source - spot_after + REACH, REACH)
        return lacking, 2 * REACH - 1 - lacking * (source - spot_after)

    def pass_on(slot, piece):
        lacking, into = passing(slot)
        copy = pltpu.make_async_remote_copy(
            src_ref=kv.at[slot, piece],
            dst_ref=kv.at[into, piece],
            send_sem=pass_sem.at[slot],
            recv_sem=recv_sem.at[into, piece],
            device_id=after,
            device_id_type=MESH,
        )
        return lacking == 1, copy

    def start_pass(slot, piece):
        lacking, copy = pass_on(slot, piece)
        pl.when(lacking)(copy.start)

    def first_sends(piece):
        send(0, 1, piece, above).start()
        send(0, REACH - 1, piece, below).start()

    def piece_at(i):
        half = lax.rem(core + lax.div(i, own_pieces), 2)
        return half * own_pieces + lax.rem(i, own_pieces)

    for i in range(own_pieces):
        to_pair(i).start()
    for i in range(own_pieces):
        pl.when(core == 0)(functools.partial(first_sends, i))
        start_pass(0, core * own_pieces + i)
    for copy in q_remote:
        copy.start()
    for i in range(own_pieces):
        piece = other * own_pieces + i
        incoming(0, piece).wait_recv()
        pl.when(core == 1)(functools.partial(first_sends, own_pieces + i))
        pl.when(core == 0)(functools.partial(first_sends, piece))
        start_pass(0, piece)
    for i in range(own_pieces):
        pl.when(core == 1)(functools.partial(first_sends, i))

    len_copy.wait()
    place = node * rows + lax.broadcasted_iota(jnp.int32, (8, tall), 1) // group

    def add_doc(j, carry):
        end, begin = carry
        end = end + lens[j]
        return end, jnp.where(place >= end, end, begin)

    _, begin = lax.fori_loop(0, docs, add_doc, (jnp.int32(0), jnp.zeros((8, tall), jnp.int32)))

    backs = [(0, 0)] + [(order[2 * i], order[2 * i + 1]) for i in range(depth)]
    key_row = lax.broadcasted_iota(jnp.int32, (8, tall), 0)
    for step, both in enumerate(backs):
        for part in range(1 if step == 0 else 2):
            base = (node - both[part]) * rows

            def fill(i, carry, step=step, part=part, base=base):
                seen = base + i * 8 + key_row
                allowed = (seen >= begin) & (seen <= place)
                at = pl.multiple_of(part * rows + i * 8, 8)
                bias[step, pl.ds(at, 8), :] = jnp.where(allowed, 0.0, MASKED)
                return carry

            lax.fori_loop(0, rows // 8, fill, 0)

    def slot_of(back):
        return back + (REACH - 1) * lax.div(back - spot + REACH - 1, REACH)

    def attend(step, piece, backs, last):
        first = not backs
        for back in backs:
            pl.when(back > spot)(incoming(REACH - 1 + back, piece).wait_recv)
        slots = [slot_of(back) for back in backs] or [0]
        depth_keys = rows * len(slots)
        for i in range(piece_heads):
            head = piece * piece_heads + i
            keys = jnp.concatenate([kv[s, piece, i, 0] for s in slots], axis=0)
            values = jnp.concatenate([kv[s, piece, i, 1] for s in slots], axis=0)
            scores = jnp.dot(keys, q_turned[head], preferred_element_type=jnp.float32)
            scores = scores * scale + bias[step, :depth_keys]
            updated = jnp.max(scores, axis=0, keepdims=True)
            if not first:
                earlier = largest[head]
                updated = jnp.maximum(earlier, updated)
                shrink = jnp.exp2(earlier - updated)
            weights = jnp.exp2(scores - updated)
            sums = jnp.sum(weights, axis=0, keepdims=True)
            out = lax.dot_general(
                values,
                weights.astype(jnp.bfloat16),
                (((0,), (0,)), ((), ())),
                preferred_element_type=jnp.float32,
            )
            if not first:
                sums = total[head] * shrink + sums
                out = acc[head] * shrink + out
            if last:
                result = (out * (1.0 / sums)).T.reshape(rows, group, width).astype(jnp.bfloat16)
                o_ref[:, pl.ds(pl.multiple_of(head * group, group), group), :] = result
            else:
                acc[head] = out
                total[head] = sums
                largest[head] = updated

    def forward(step, piece):
        incoming(step, piece).wait_recv()
        pl.when(step < depth)(lambda: send(step, step + 1, piece, above).start())
        start_pass(step, piece)

        @pl.when(step < depth)
        def _():
            incoming(REACH - step, piece).wait_recv()
            pl.when(step < depth - 1)(
                lambda: send(REACH - step, REACH - step - 1, piece, below).start()
            )
            start_pass(REACH - step, piece)

    def turn(head):
        q_turned[head] = q_scr.reshape(heads, tall, width)[head].T

    for k in range(kv_heads):
        q_local[k].wait()
    for k in range(kv_heads):
        pltpu.make_async_remote_copy(
            src_ref=q_scr.at[other * kv_heads + k],
            dst_ref=q_scr.at[other * kv_heads + k],
            send_sem=q_send_sem.at[k],
            recv_sem=q_sem.at[other, k],
            device_id=pair,
            device_id_type=MESH,
        ).wait_recv()

    def begin_piece(i, carry):
        piece = piece_at(i)
        forward(1, piece)
        for k in range(piece_heads):
            turn(piece * piece_heads + k)
        attend(0, piece, (), False)
        return carry

    lax.fori_loop(0, PIECES, begin_piece, 0)

    def middle(i, carry):
        step, piece = lax.div(i, PIECES) + 1, piece_at(lax.rem(i, PIECES))
        forward(step + 1, piece)
        both = [
            sum(equal(step, at) * backs[at][part] for at in range(1, depth)) for part in range(2)
        ]
        attend(step, piece, both, False)
        return carry

    lax.fori_loop(0, (depth - 1) * PIECES, middle, 0)

    def sent(block, sem):
        pltpu.make_async_remote_copy(
            src_ref=block,
            dst_ref=block,
            send_sem=sem,
            recv_sem=recv_sem.at[0, 0],
            device_id=pair,
            device_id_type=MESH,
        ).wait_send()

    def sent_on(slot):
        lacking, _ = passing(slot)
        pl.when(lacking == 1)(functools.partial(sent, kv.at[slot], pass_sem.at[slot]))

    sent(kv_out, pair_sem)
    for copy in q_remote:
        copy.wait_send()
    for slot in (1, 2, 3, 6, 7):
        sent(kv.at[slot], send_sem.at[slot])
    for slot in (0, 1, 2, 6, 7):
        sent_on(slot)

    def finish_piece(i, carry):
        attend(depth, piece_at(i), backs[depth], True)
        return carry

    lax.fori_loop(0, PIECES, finish_piece, 0)

    for slot in (4, 5):
        sent(kv.at[slot], send_sem.at[slot])
    for slot in (3, 4, 5):
        sent_on(slot)


def shards(queries, key_heads, value_head_rows, doc_lengths):
    queries, key_heads, value_head_rows, doc_lengths = (
        pltpu.with_memory_space_constraint(a, pltpu.HBM)
        for a in (queries, key_heads, value_head_rows, doc_lengths)
    )
    kv_heads = key_heads.shape[1]
    rows = key_heads.shape[0] // 2
    width = key_heads.shape[2]
    group = queries.shape[1] // kv_heads
    heads = 2 * kv_heads
    tall = rows * group
    piece = (heads // PIECES, 2, rows, width)
    steps = REACH // 2 + 1
    any_space = pl.BlockSpec(memory_space=pl.ANY)
    return pl.pallas_call(
        functools.partial(kernel, lax.axis_size("ctx")),
        name="relay_attention",
        out_shape=jax.ShapeDtypeStruct((rows, heads * group, width), jnp.bfloat16),
        in_specs=[any_space] * 4,
        out_specs=pl.BlockSpec(memory_space=pltpu.VMEM),
        scratch_shapes=[
            pltpu.VMEM((heads, rows, group, width), jnp.bfloat16),
            pltpu.VMEM((heads, width, tall), jnp.bfloat16),
            pltpu.VMEM((2 * REACH, PIECES, *piece), jnp.bfloat16),
            pltpu.VMEM((PIECES // 2, *piece), jnp.bfloat16),
            pltpu.VMEM((2, 2, rows, kv_heads, width), jnp.bfloat16),
            pltpu.VMEM((rows, kv_heads, width), jnp.float32),
            pltpu.VMEM((steps, 2 * rows, tall), jnp.float32),
            pltpu.VMEM((heads, width, tall), jnp.float32),
            pltpu.VMEM((heads, 1, tall), jnp.float32),
            pltpu.VMEM((heads, 1, tall), jnp.float32),
            pltpu.SMEM(doc_lengths.shape, jnp.int32),
            pltpu.SemaphoreType.DMA((2, 2)),
            pltpu.SemaphoreType.DMA,
            pltpu.SemaphoreType.DMA((2, kv_heads)),
            pltpu.SemaphoreType.DMA((kv_heads,)),
            pltpu.SemaphoreType.DMA((2 * REACH, PIECES)),
            pltpu.SemaphoreType.DMA((REACH,)),
            pltpu.SemaphoreType.DMA((REACH,)),
            pltpu.SemaphoreType.DMA,
        ],
        compiler_params=pltpu.CompilerParams(
            collective_id=0, has_side_effects=True, vmem_limit_bytes=32 << 20
        ),
    )(queries, key_heads, value_head_rows, doc_lengths)


def solution(mesh):
    in_specs = (P("ctx", "head", None), P("ctx", "head", None), P("ctx", "head", None), P())
    out_specs = P(("ctx", "head"), None, None)
    return jax.shard_map(shards, mesh=mesh, in_specs=in_specs, out_specs=out_specs, check_vma=False)
```

```python
import functools
import math

import jax
import jax.numpy as jnp
from jax import lax
from jax.experimental import pallas as pl
from jax.experimental.pallas import tpu as pltpu
from jax.sharding import PartitionSpec as P

REACH = 8
MASKED = -1e30
PIECES = 4
MESH = pl.DeviceIdType.MESH

USUAL = (1, 8, 2, 7, 3, 6, 4, 5)
AT_FOLD = (
    USUAL,
    (3, 1, 2, 4, 5, 6, 8, 7),
    (5, 1, 4, 6, 2, 3, 7, 8),
    (7, 1, 6, 8, 2, 5, 3, 4),
    USUAL,
    (1, 2, 3, 5, 6, 8, 4, 7),
    (1, 2, 6, 7, 3, 5, 8, 4),
    USUAL,
)


def kernel(
    ctx_count,
    q_hbm,
    k_hbm,
    v_hbm,
    len_hbm,
    o_ref,
    q_scr,
    q_turned,
    kv,
    kv_out,
    raw,
    wide,
    bias,
    acc,
    total,
    largest,
    lens,
    raw_sem,
    len_sem,
    q_sem,
    q_send_sem,
    recv_sem,
    send_sem,
    pass_sem,
    pair_sem,
):
    kv_heads = k_hbm.shape[1]
    heads = 2 * kv_heads
    group = q_hbm.shape[1] // kv_heads
    rows = k_hbm.shape[0] // 2
    width = k_hbm.shape[2]
    docs = len_hbm.shape[0]
    tall = rows * group
    nodes = 2 * ctx_count
    own_pieces = PIECES // 2
    piece_heads = heads // PIECES
    depth = REACH // 2
    scale = math.log2(math.e) / math.sqrt(width)

    chip = lax.axis_index("ctx")
    core = lax.axis_index("head")
    other = 1 - core
    node = chip + core * (nodes - 1 - 2 * chip)
    ring, spot = lax.div(node, REACH), lax.rem(node, REACH)
    rings = ctx_count // REACH
    along = lax.rem(ring, rings)
    folds = lax.div(along + 1, rings)
    folded = 1 - lax.div(along + rings - 1, rings)

    def device(n):
        leg = lax.div(n, ctx_count)
        return (n + leg * (nodes - 1 - 2 * n), leg)

    pair = (chip, other)
    above = device(ring * REACH + lax.rem(spot + 1, REACH))
    below = device(ring * REACH + lax.rem(spot + REACH - 1, REACH))
    opposite = nodes - 1 - node
    after = device(folds * opposite + (1 - folds) * lax.rem(node + REACH, nodes))
    before = device(folded * opposite + (1 - folded) * lax.rem(node + nodes - REACH, nodes))
    spot_after = spot + folds * (REACH - 1 - 2 * spot)

    def equal(a, b):
        return 1 - lax.div((a - b) * (a - b) + 63, 64)

    order = []
    for i in range(REACH):
        change = sum(
            equal(spot, place) * (AT_FOLD[place][i] - USUAL[i])
            for place in range(REACH)
            if AT_FOLD[place][i] != USUAL[i]
        )
        order.append(USUAL[i] + folded * change)

    local = []
    for part, half in enumerate((core, other)):
        for which, source in enumerate((k_hbm, v_hbm)):
            copy = pltpu.make_async_copy(
                source.at[pl.ds(pl.multiple_of(half * rows, rows), rows)],
                raw.at[part, which],
                raw_sem.at[part, which],
            )
            copy.start()
            local.append(copy)
    len_copy = pltpu.make_async_copy(len_hbm, lens, len_sem)
    len_copy.start()
    q_local, q_remote = [], []
    for k in range(kv_heads):
        copy = pltpu.make_async_copy(
            q_hbm.at[pl.ds(pl.multiple_of(core * rows, rows), rows), pl.ds(k * group, group)],
            q_scr.at[core * kv_heads + k],
            q_sem.at[core, k],
        )
        copy.start()
        q_local.append(copy)
        q_remote.append(
            pltpu.make_async_remote_copy(
                src_ref=q_hbm.at[
                    pl.ds(pl.multiple_of(other * rows, rows), rows), pl.ds(k * group, group)
                ],
                dst_ref=q_scr.at[core * kv_heads + k],
                send_sem=q_send_sem.at[k],
                recv_sem=q_sem.at[core, k],
                device_id=pair,
                device_id_type=MESH,
            )
        )

    barrier = pltpu.get_barrier_semaphore()
    for target in (pair, above, below, before):
        pl.semaphore_signal(barrier, inc=1, device_id=target, device_id_type=MESH)

    for part in (1, 0):
        for which in range(2):
            local[2 * part + which].wait()
            wide[...] = raw[part, which].astype(jnp.float32)
            for k in range(kv_heads):
                block = wide.reshape(rows * kv_heads, width)[
                    pl.ds(k, rows, stride=kv_heads), :
                ].astype(jnp.bfloat16)
                piece, head = k // piece_heads, k % piece_heads
                if part == 0:
                    kv[0, core * own_pieces + piece, head, which] = block
                else:
                    kv_out[piece, head, which] = block

    pl.semaphore_wait(barrier, 4)

    def to_pair(i):
        return pltpu.make_async_remote_copy(
            src_ref=kv_out.at[i],
            dst_ref=kv.at[0, core * own_pieces + i],
            send_sem=pair_sem,
            recv_sem=recv_sem.at[0, core * own_pieces + i],
            device_id=pair,
            device_id_type=MESH,
        )

    def send(slot, into, piece, target):
        return pltpu.make_async_remote_copy(
            src_ref=kv.at[slot, piece],
            dst_ref=kv.at[into, piece],
            send_sem=send_sem.at[into],
            recv_sem=recv_sem.at[into, piece],
            device_id=target,
            device_id_type=MESH,
        )

    def incoming(slot, piece):
        return pltpu.make_async_remote_copy(
            src_ref=kv.at[slot, piece],
            dst_ref=kv.at[slot, piece],
            send_sem=pair_sem,
            recv_sem=recv_sem.at[slot, piece],
            device_id=above,
            device_id_type=MESH,
        )

    def passing(slot):
        source = lax.rem(spot - slot + REACH, REACH)
        lacking = lax.div(source - spot_after + REACH, REACH)
        return lacking, 2 * REACH - 1 - lacking * (source - spot_after)

    def pass_on(slot, piece):
        lacking, into = passing(slot)
        copy = pltpu.make_async_remote_copy(
            src_ref=kv.at[slot, piece],
            dst_ref=kv.at[into, piece],
            send_sem=pass_sem.at[slot],
            recv_sem=recv_sem.at[into, piece],
            device_id=after,
            device_id_type=MESH,
        )
        return lacking == 1, copy

    def start_pass(slot, piece):
        lacking, copy = pass_on(slot, piece)
        pl.when(lacking)(copy.start)

    def first_sends(piece):
        send(0, 1, piece, above).start()
        send(0, REACH - 1, piece, below).start()

    def piece_at(i):
        half = lax.rem(core + lax.div(i, own_pieces), 2)
        return half * own_pieces + lax.rem(i, own_pieces)

    for i in range(own_pieces):
        to_pair(i).start()
    for i in range(own_pieces):
        pl.when(core == 0)(functools.partial(first_sends, i))
        start_pass(0, core * own_pieces + i)
    for copy in q_remote:
        copy.start()
    for i in range(own_pieces):
        piece = other * own_pieces + i
        incoming(0, piece).wait_recv()
        pl.when(core == 0)(functools.partial(first_sends, piece))
        start_pass(0, piece)
    for i in range(PIECES):
        pl.when(core == 1)(functools.partial(first_sends, piece_at(i)))

    len_copy.wait()
    place = node * rows + lax.broadcasted_iota(jnp.int32, (8, tall), 1) // group

    def add_doc(j, carry):
        end, begin = carry
        end = end + lens[j]
        return end, jnp.where(place >= end, end, begin)

    _, begin = lax.fori_loop(0, docs, add_doc, (jnp.int32(0), jnp.zeros((8, tall), jnp.int32)))

    backs = [(0, 0)] + [(order[2 * i], order[2 * i + 1]) for i in range(depth)]
    key_row = lax.broadcasted_iota(jnp.int32, (8, tall), 0)
    for step, both in enumerate(backs):
        for part in range(1 if step == 0 else 2):
            base = (node - both[part]) * rows

            def fill(i, carry, step=step, part=part, base=base):
                seen = base + i * 8 + key_row
                allowed = (seen >= begin) & (seen <= place)
                at = pl.multiple_of(part * rows + i * 8, 8)
                bias[step, pl.ds(at, 8), :] = jnp.where(allowed, 0.0, MASKED)
                return carry

            lax.fori_loop(0, rows // 8, fill, 0)

    def slot_of(back):
        return back + (REACH - 1) * lax.div(back - spot + REACH - 1, REACH)

    def attend(step, piece, backs, last):
        first = not backs
        for back in backs:
            pl.when(back > spot)(incoming(REACH - 1 + back, piece).wait_recv)
        slots = [slot_of(back) for back in backs] or [0]
        depth_keys = rows * len(slots)
        for i in range(piece_heads):
            head = piece * piece_heads + i
            keys = jnp.concatenate([kv[s, piece, i, 0] for s in slots], axis=0)
            values = jnp.concatenate([kv[s, piece, i, 1] for s in slots], axis=0)
            scores = jnp.dot(keys, q_turned[head], preferred_element_type=jnp.float32)
            scores = scores * scale + bias[step, :depth_keys]
            updated = jnp.max(scores, axis=0, keepdims=True)
            if not first:
                earlier = largest[head]
                updated = jnp.maximum(earlier, updated)
                shrink = jnp.exp2(earlier - updated)
            weights = jnp.exp2(scores - updated)
            sums = jnp.sum(weights, axis=0, keepdims=True)
            out = lax.dot_general(
                values,
                weights.astype(jnp.bfloat16),
                (((0,), (0,)), ((), ())),
                preferred_element_type=jnp.float32,
            )
            if not first:
                sums = total[head] * shrink + sums
                out = acc[head] * shrink + out
            if last:
                result = (out * (1.0 / sums)).T.reshape(rows, group, width).astype(jnp.bfloat16)
                o_ref[:, pl.ds(pl.multiple_of(head * group, group), group), :] = result
            else:
                acc[head] = out
                total[head] = sums
                largest[head] = updated

    def forward(step, piece):
        incoming(step, piece).wait_recv()
        pl.when(step < depth)(lambda: send(step, step + 1, piece, above).start())
        start_pass(step, piece)

        @pl.when(step < depth)
        def _():
            incoming(REACH - step, piece).wait_recv()
            pl.when(step < depth - 1)(
                lambda: send(REACH - step, REACH - step - 1, piece, below).start()
            )
            start_pass(REACH - step, piece)

    def turn(head):
        q_turned[head] = q_scr.reshape(heads, tall, width)[head].T

    for k in range(kv_heads):
        q_local[k].wait()
    for k in range(kv_heads):
        pltpu.make_async_remote_copy(
            src_ref=q_scr.at[other * kv_heads + k],
            dst_ref=q_scr.at[other * kv_heads + k],
            send_sem=q_send_sem.at[k],
            recv_sem=q_sem.at[other, k],
            device_id=pair,
            device_id_type=MESH,
        ).wait_recv()

    def begin_piece(i, carry):
        piece = piece_at(i)
        forward(1, piece)
        for k in range(piece_heads):
            turn(piece * piece_heads + k)
        attend(0, piece, (), False)
        return carry

    lax.fori_loop(0, PIECES, begin_piece, 0)

    def middle(i, carry):
        step, piece = lax.div(i, PIECES) + 1, piece_at(lax.rem(i, PIECES))
        forward(step + 1, piece)
        both = [
            sum(equal(step, at) * backs[at][part] for at in range(1, depth)) for part in range(2)
        ]
        attend(step, piece, both, False)
        return carry

    lax.fori_loop(0, (depth - 1) * PIECES, middle, 0)

    def sent(block, sem):
        pltpu.make_async_remote_copy(
            src_ref=block,
            dst_ref=block,
            send_sem=sem,
            recv_sem=recv_sem.at[0, 0],
            device_id=pair,
            device_id_type=MESH,
        ).wait_send()

    def sent_on(slot):
        lacking, _ = passing(slot)
        pl.when(lacking == 1)(functools.partial(sent, kv.at[slot], pass_sem.at[slot]))

    sent(kv_out, pair_sem)
    for copy in q_remote:
        copy.wait_send()
    for slot in (1, 2, 3, 6, 7):
        sent(kv.at[slot], send_sem.at[slot])
    for slot in (0, 1, 2, 6, 7):
        sent_on(slot)

    def finish_piece(i, carry):
        attend(depth, piece_at(i), backs[depth], True)
        return carry

    lax.fori_loop(0, PIECES, finish_piece, 0)

    for slot in (4, 5):
        sent(kv.at[slot], send_sem.at[slot])
    for slot in (3, 4, 5):
        sent_on(slot)


def shards(queries, key_heads, value_head_rows, doc_lengths):
    queries, key_heads, value_head_rows, doc_lengths = (
        pltpu.with_memory_space_constraint(a, pltpu.HBM)
        for a in (queries, key_heads, value_head_rows, doc_lengths)
    )
    kv_heads = key_heads.shape[1]
    rows = key_heads.shape[0] // 2
    width = key_heads.shape[2]
    group = queries.shape[1] // kv_heads
    heads = 2 * kv_heads
    tall = rows * group
    piece = (heads // PIECES, 2, rows, width)
    steps = REACH // 2 + 1
    any_space = pl.BlockSpec(memory_space=pl.ANY)
    return pl.pallas_call(
        functools.partial(kernel, lax.axis_size("ctx")),
        name="relay_attention",
        out_shape=jax.ShapeDtypeStruct((rows, heads * group, width), jnp.bfloat16),
        in_specs=[any_space] * 4,
        out_specs=pl.BlockSpec(memory_space=pltpu.VMEM),
        scratch_shapes=[
            pltpu.VMEM((heads, rows, group, width), jnp.bfloat16),
            pltpu.VMEM((heads, width, tall), jnp.bfloat16),
            pltpu.VMEM((2 * REACH, PIECES, *piece), jnp.bfloat16),
            pltpu.VMEM((PIECES // 2, *piece), jnp.bfloat16),
            pltpu.VMEM((2, 2, rows, kv_heads, width), jnp.bfloat16),
            pltpu.VMEM((rows, kv_heads, width), jnp.float32),
            pltpu.VMEM((steps, 2 * rows, tall), jnp.float32),
            pltpu.VMEM((heads, width, tall), jnp.float32),
            pltpu.VMEM((heads, 1, tall), jnp.float32),
            pltpu.VMEM((heads, 1, tall), jnp.float32),
            pltpu.SMEM(doc_lengths.shape, jnp.int32),
            pltpu.SemaphoreType.DMA((2, 2)),
            pltpu.SemaphoreType.DMA,
            pltpu.SemaphoreType.DMA((2, kv_heads)),
            pltpu.SemaphoreType.DMA((kv_heads,)),
            pltpu.SemaphoreType.DMA((2 * REACH, PIECES)),
            pltpu.SemaphoreType.DMA((REACH,)),
            pltpu.SemaphoreType.DMA((REACH,)),
            pltpu.SemaphoreType.DMA,
        ],
        compiler_params=pltpu.CompilerParams(
            collective_id=0, has_side_effects=True, vmem_limit_bytes=32 << 20
        ),
    )(queries, key_heads, value_head_rows, doc_lengths)


def solution(mesh):
    in_specs = (P("ctx", "head", None), P("ctx", "head", None), P("ctx", "head", None), P())
    out_specs = P(("ctx", "head"), None, None)
    return jax.shard_map(shards, mesh=mesh, in_specs=in_specs, out_specs=out_specs, check_vma=False)
```

```python
import functools
import math

import jax
import jax.numpy as jnp
from jax import lax
from jax.experimental import pallas as pl
from jax.experimental.pallas import tpu as pltpu
from jax.sharding import PartitionSpec as P

REACH = 8
MASKED = -1e30
PIECES = 4
MESH = pl.DeviceIdType.MESH

USUAL = (1, 8, 2, 7, 3, 6, 4, 5)
AT_FOLD = (
    USUAL,
    (3, 1, 2, 4, 5, 6, 8, 7),
    (5, 1, 4, 6, 2, 3, 7, 8),
    (7, 1, 6, 8, 2, 5, 3, 4),
    USUAL,
    (1, 2, 3, 5, 6, 8, 4, 7),
    (1, 2, 6, 7, 3, 5, 8, 4),
    USUAL,
)


def kernel(
    ctx_count,
    q_hbm,
    k_hbm,
    v_hbm,
    len_hbm,
    o_ref,
    q_scr,
    q_turned,
    kv,
    kv_out,
    raw,
    wide,
    bias,
    acc,
    total,
    largest,
    lens,
    raw_sem,
    len_sem,
    q_sem,
    q_send_sem,
    recv_sem,
    send_sem,
    pass_sem,
    pair_sem,
    lead_sem,
):
    kv_heads = k_hbm.shape[1]
    heads = 2 * kv_heads
    group = q_hbm.shape[1] // kv_heads
    rows = k_hbm.shape[0] // 2
    width = k_hbm.shape[2]
    docs = len_hbm.shape[0]
    tall = rows * group
    nodes = 2 * ctx_count
    own_pieces = PIECES // 2
    piece_heads = heads // PIECES
    depth = REACH // 2
    scale = math.log2(math.e) / math.sqrt(width)

    chip = lax.axis_index("ctx")
    core = lax.axis_index("head")
    other = 1 - core
    node = chip + core * (nodes - 1 - 2 * chip)
    ring, spot = lax.div(node, REACH), lax.rem(node, REACH)
    rings = ctx_count // REACH
    along = lax.rem(ring, rings)
    folds = lax.div(along + 1, rings)
    folded = 1 - lax.div(along + rings - 1, rings)

    def device(n):
        leg = lax.div(n, ctx_count)
        return (n + leg * (nodes - 1 - 2 * n), leg)

    pair = (chip, other)
    above = device(ring * REACH + lax.rem(spot + 1, REACH))
    below = device(ring * REACH + lax.rem(spot + REACH - 1, REACH))
    opposite = nodes - 1 - node
    after = device(folds * opposite + (1 - folds) * lax.rem(node + REACH, nodes))
    before = device(folded * opposite + (1 - folded) * lax.rem(node + nodes - REACH, nodes))
    spot_after = spot + folds * (REACH - 1 - 2 * spot)

    def equal(a, b):
        return 1 - lax.div((a - b) * (a - b) + 63, 64)

    order = []
    for i in range(REACH):
        change = sum(
            equal(spot, place) * (AT_FOLD[place][i] - USUAL[i])
            for place in range(REACH)
            if AT_FOLD[place][i] != USUAL[i]
        )
        order.append(USUAL[i] + folded * change)

    local = []
    for part, half in enumerate((core, other)):
        for which, source in enumerate((k_hbm, v_hbm)):
            copy = pltpu.make_async_copy(
                source.at[pl.ds(pl.multiple_of(half * rows, rows), rows)],
                raw.at[part, which],
                raw_sem.at[part, which],
            )
            copy.start()
            local.append(copy)
    len_copy = pltpu.make_async_copy(len_hbm, lens, len_sem)
    len_copy.start()
    q_local, q_remote = [], []
    for k in range(kv_heads):
        copy = pltpu.make_async_copy(
            q_hbm.at[pl.ds(pl.multiple_of(core * rows, rows), rows), pl.ds(k * group, group)],
            q_scr.at[core * kv_heads + k],
            q_sem.at[core, k],
        )
        copy.start()
        q_local.append(copy)
        q_remote.append(
            pltpu.make_async_remote_copy(
                src_ref=q_hbm.at[
                    pl.ds(pl.multiple_of(other * rows, rows), rows), pl.ds(k * group, group)
                ],
                dst_ref=q_scr.at[core * kv_heads + k],
                send_sem=q_send_sem.at[k],
                recv_sem=q_sem.at[core, k],
                device_id=pair,
                device_id_type=MESH,
            )
        )

    barrier = pltpu.get_barrier_semaphore()
    for target in (pair, above, below, before):
        pl.semaphore_signal(barrier, inc=1, device_id=target, device_id_type=MESH)

    for part in (1, 0):
        for which in range(2):
            local[2 * part + which].wait()
            wide[...] = raw[part, which].astype(jnp.float32)
            for k in range(kv_heads):
                block = wide.reshape(rows * kv_heads, width)[
                    pl.ds(k, rows, stride=kv_heads), :
                ].astype(jnp.bfloat16)
                piece, head = k // piece_heads, k % piece_heads
                if part == 0:
                    kv[0, core * own_pieces + piece, head, which] = block
                else:
                    kv_out[piece, head, which] = block

    pl.semaphore_wait(barrier, 4)

    def to_pair(i):
        return pltpu.make_async_remote_copy(
            src_ref=kv_out.at[i],
            dst_ref=kv.at[0, core * own_pieces + i],
            send_sem=pair_sem,
            recv_sem=recv_sem.at[0, core * own_pieces + i],
            device_id=pair,
            device_id_type=MESH,
        )

    def send(slot, into, piece, target):
        return pltpu.make_async_remote_copy(
            src_ref=kv.at[slot, piece],
            dst_ref=kv.at[into, piece],
            send_sem=send_sem.at[into],
            recv_sem=recv_sem.at[into, piece],
            device_id=target,
            device_id_type=MESH,
        )

    def incoming(slot, piece):
        return pltpu.make_async_remote_copy(
            src_ref=kv.at[slot, piece],
            dst_ref=kv.at[slot, piece],
            send_sem=pair_sem,
            recv_sem=recv_sem.at[slot, piece],
            device_id=above,
            device_id_type=MESH,
        )

    def passing(slot):
        source = lax.rem(spot - slot + REACH, REACH)
        lacking = lax.div(source - spot_after + REACH, REACH)
        return lacking, 2 * REACH - 1 - lacking * (source - spot_after)

    def pass_on(slot, piece):
        lacking, into = passing(slot)
        copy = pltpu.make_async_remote_copy(
            src_ref=kv.at[slot, piece],
            dst_ref=kv.at[into, piece],
            send_sem=pass_sem.at[slot],
            recv_sem=recv_sem.at[into, piece],
            device_id=after,
            device_id_type=MESH,
        )
        return lacking == 1, copy

    def start_pass(slot, piece):
        lacking, copy = pass_on(slot, piece)
        pl.when(lacking)(copy.start)

    def first_sends(piece):
        send(0, 1, piece, above).start()
        send(0, REACH - 1, piece, below).start()

    def piece_at(i):
        half = lax.rem(core + lax.div(i, own_pieces), 2)
        return half * own_pieces + lax.rem(i, own_pieces)

    for i in range(own_pieces):
        to_pair(i).start()
    for i in range(own_pieces):
        pl.when(core == 0)(functools.partial(first_sends, i))
        start_pass(0, core * own_pieces + i)
    for copy in q_remote:
        copy.start()
    for i in range(own_pieces):
        piece = other * own_pieces + i
        incoming(0, piece).wait_recv()
        pl.when(core == 0)(functools.partial(first_sends, piece))
        start_pass(0, piece)
    @pl.when(core == 0)
    def _():
        pl.semaphore_signal(lead_sem, inc=1, device_id=pair, device_id_type=MESH)

    @pl.when(core == 1)
    def _():
        pl.semaphore_wait(lead_sem, 1)
        for i in range(PIECES):
            first_sends(piece_at(i))


    len_copy.wait()
    place = node * rows + lax.broadcasted_iota(jnp.int32, (8, tall), 1) // group

    def add_doc(j, carry):
        end, begin = carry
        end = end + lens[j]
        return end, jnp.where(place >= end, end, begin)

    _, begin = lax.fori_loop(0, docs, add_doc, (jnp.int32(0), jnp.zeros((8, tall), jnp.int32)))

    backs = [(0, 0)] + [(order[2 * i], order[2 * i + 1]) for i in range(depth)]
    key_row = lax.broadcasted_iota(jnp.int32, (8, tall), 0)
    for step, both in enumerate(backs):
        for part in range(1 if step == 0 else 2):
            base = (node - both[part]) * rows

            def fill(i, carry, step=step, part=part, base=base):
                seen = base + i * 8 + key_row
                allowed = (seen >= begin) & (seen <= place)
                at = pl.multiple_of(part * rows + i * 8, 8)
                bias[step, pl.ds(at, 8), :] = jnp.where(allowed, 0.0, MASKED)
                return carry

            lax.fori_loop(0, rows // 8, fill, 0)

    def slot_of(back):
        return back + (REACH - 1) * lax.div(back - spot + REACH - 1, REACH)

    def attend(step, piece, backs, last):
        first = not backs
        for back in backs:
            pl.when(back > spot)(incoming(REACH - 1 + back, piece).wait_recv)
        slots = [slot_of(back) for back in backs] or [0]
        depth_keys = rows * len(slots)
        for i in range(piece_heads):
            head = piece * piece_heads + i
            keys = jnp.concatenate([kv[s, piece, i, 0] for s in slots], axis=0)
            values = jnp.concatenate([kv[s, piece, i, 1] for s in slots], axis=0)
            scores = jnp.dot(keys, q_turned[head], preferred_element_type=jnp.float32)
            scores = scores * scale + bias[step, :depth_keys]
            updated = jnp.max(scores, axis=0, keepdims=True)
            if not first:
                earlier = largest[head]
                updated = jnp.maximum(earlier, updated)
                shrink = jnp.exp2(earlier - updated)
            weights = jnp.exp2(scores - updated)
            sums = jnp.sum(weights, axis=0, keepdims=True)
            out = lax.dot_general(
                values,
                weights.astype(jnp.bfloat16),
                (((0,), (0,)), ((), ())),
                preferred_element_type=jnp.float32,
            )
            if not first:
                sums = total[head] * shrink + sums
                out = acc[head] * shrink + out
            if last:
                result = (out * (1.0 / sums)).T.reshape(rows, group, width).astype(jnp.bfloat16)
                o_ref[:, pl.ds(pl.multiple_of(head * group, group), group), :] = result
            else:
                acc[head] = out
                total[head] = sums
                largest[head] = updated

    def forward(step, piece):
        incoming(step, piece).wait_recv()
        pl.when(step < depth)(lambda: send(step, step + 1, piece, above).start())
        start_pass(step, piece)

        @pl.when(step < depth)
        def _():
            incoming(REACH - step, piece).wait_recv()
            pl.when(step < depth - 1)(
                lambda: send(REACH - step, REACH - step - 1, piece, below).start()
            )
            start_pass(REACH - step, piece)

    def turn(head):
        q_turned[head] = q_scr.reshape(heads, tall, width)[head].T

    for k in range(kv_heads):
        q_local[k].wait()
    for k in range(kv_heads):
        pltpu.make_async_remote_copy(
            src_ref=q_scr.at[other * kv_heads + k],
            dst_ref=q_scr.at[other * kv_heads + k],
            send_sem=q_send_sem.at[k],
            recv_sem=q_sem.at[other, k],
            device_id=pair,
            device_id_type=MESH,
        ).wait_recv()

    def begin_piece(i, carry):
        piece = piece_at(i)
        forward(1, piece)
        for k in range(piece_heads):
            turn(piece * piece_heads + k)
        attend(0, piece, (), False)
        return carry

    lax.fori_loop(0, PIECES, begin_piece, 0)

    def middle(i, carry):
        step, piece = lax.div(i, PIECES) + 1, piece_at(lax.rem(i, PIECES))
        forward(step + 1, piece)
        both = [
            sum(equal(step, at) * backs[at][part] for at in range(1, depth)) for part in range(2)
        ]
        attend(step, piece, both, False)
        return carry

    lax.fori_loop(0, (depth - 1) * PIECES, middle, 0)

    def sent(block, sem):
        pltpu.make_async_remote_copy(
            src_ref=block,
            dst_ref=block,
            send_sem=sem,
            recv_sem=recv_sem.at[0, 0],
            device_id=pair,
            device_id_type=MESH,
        ).wait_send()

    def sent_on(slot):
        lacking, _ = passing(slot)
        pl.when(lacking == 1)(functools.partial(sent, kv.at[slot], pass_sem.at[slot]))

    sent(kv_out, pair_sem)
    for copy in q_remote:
        copy.wait_send()
    for slot in (1, 2, 3, 6, 7):
        sent(kv.at[slot], send_sem.at[slot])
    for slot in (0, 1, 2, 6, 7):
        sent_on(slot)

    def finish_piece(i, carry):
        attend(depth, piece_at(i), backs[depth], True)
        return carry

    lax.fori_loop(0, PIECES, finish_piece, 0)

    for slot in (4, 5):
        sent(kv.at[slot], send_sem.at[slot])
    for slot in (3, 4, 5):
        sent_on(slot)


def shards(queries, key_heads, value_head_rows, doc_lengths):
    queries, key_heads, value_head_rows, doc_lengths = (
        pltpu.with_memory_space_constraint(a, pltpu.HBM)
        for a in (queries, key_heads, value_head_rows, doc_lengths)
    )
    kv_heads = key_heads.shape[1]
    rows = key_heads.shape[0] // 2
    width = key_heads.shape[2]
    group = queries.shape[1] // kv_heads
    heads = 2 * kv_heads
    tall = rows * group
    piece = (heads // PIECES, 2, rows, width)
    steps = REACH // 2 + 1
    any_space = pl.BlockSpec(memory_space=pl.ANY)
    return pl.pallas_call(
        functools.partial(kernel, lax.axis_size("ctx")),
        name="relay_attention",
        out_shape=jax.ShapeDtypeStruct((rows, heads * group, width), jnp.bfloat16),
        in_specs=[any_space] * 4,
        out_specs=pl.BlockSpec(memory_space=pltpu.VMEM),
        scratch_shapes=[
            pltpu.VMEM((heads, rows, group, width), jnp.bfloat16),
            pltpu.VMEM((heads, width, tall), jnp.bfloat16),
            pltpu.VMEM((2 * REACH, PIECES, *piece), jnp.bfloat16),
            pltpu.VMEM((PIECES // 2, *piece), jnp.bfloat16),
            pltpu.VMEM((2, 2, rows, kv_heads, width), jnp.bfloat16),
            pltpu.VMEM((rows, kv_heads, width), jnp.float32),
            pltpu.VMEM((steps, 2 * rows, tall), jnp.float32),
            pltpu.VMEM((heads, width, tall), jnp.float32),
            pltpu.VMEM((heads, 1, tall), jnp.float32),
            pltpu.VMEM((heads, 1, tall), jnp.float32),
            pltpu.SMEM(doc_lengths.shape, jnp.int32),
            pltpu.SemaphoreType.DMA((2, 2)),
            pltpu.SemaphoreType.DMA,
            pltpu.SemaphoreType.DMA((2, kv_heads)),
            pltpu.SemaphoreType.DMA((kv_heads,)),
            pltpu.SemaphoreType.DMA((2 * REACH, PIECES)),
            pltpu.SemaphoreType.DMA((REACH,)),
            pltpu.SemaphoreType.DMA((REACH,)),
            pltpu.SemaphoreType.DMA,
            pltpu.SemaphoreType.REGULAR,
        ],
        compiler_params=pltpu.CompilerParams(
            collective_id=0, has_side_effects=True, vmem_limit_bytes=32 << 20
        ),
    )(queries, key_heads, value_head_rows, doc_lengths)


def solution(mesh):
    in_specs = (P("ctx", "head", None), P("ctx", "head", None), P("ctx", "head", None), P())
    out_specs = P(("ctx", "head"), None, None)
    return jax.shard_map(shards, mesh=mesh, in_specs=in_specs, out_specs=out_specs, check_vma=False)
```
